512 devices in a mesh: mut: 32 (over x_lo, z, core), test: 16 (over x_hi, y).
Axes of the slice: x: 4 (x_hi: 2, x_lo: 2; x = x_hi * 2 + x_lo), y: 8, z: 8, core: 2. Of those that a mesh axis runs over, the one named last changes fastest.
Arguments:
- input_activation: bfloat16 [2048, 28, 1024], P(('mut', 'test')), may hold values from -18 to 18
- ground_truth_class: int32 [2048], replicated, may hold values from 0 to 999
- remaining_pictures: int32 [128, 224], P('mut', 'test'), may hold values from 0 to 127, as said below
- learned_narrowing_kernel: bfloat16 [1024, 256], replicated, may hold values from -0.1875 to 0.1875
- learned_widening_kernel: bfloat16 [256, 1024], replicated, may hold values from -0.375 to 0.375
- narrowing_perturbation: bfloat16 [128, 1024, 256], P('mut', 'test'), may hold values from -0.09375 to 0.09375
- widening_perturbation: bfloat16 [128, 256, 1024], P('mut', None, 'test'), may hold values from -0.1875 to 0.1875
- perturbation_strength: float32 [128, 2], P('mut'), may hold values from 0.25 to 2
- readout_matrix: bfloat16 [1024, 1000], replicated, may hold values from -1 to 1
Outputs:
- kill: float32 [128, 2, 224], P('mut', None, 'test')
The draws below stay inside these ranges and needn't reach their ends.
Inputs may be any that keep to these rules, and one draw needn't show every extreme that they name: `remaining_pictures`: entry t * 14 + j of a mutant's row names an image of test shard t; image i of a shard lies on the device at mut index i // 4. Among the entries of one mut index's 4 mutants in one test shard, at most 2 lie on any one device's images, and some device takes exactly 2.
All inputs are finite; a program needn't handle non-finite values.
Results may differ from the reference program's by a relative error of at most 0.0003.
Values may be sent and summed in bfloat16 or wider, within the bound.
No kernel may reach another device: no remote copies, remote signals or barrier semaphores. Data moves between devices by JAX's collectives and lax.ppermute only.
A program may use at most 64 MiB of HBM per device.

```python
import math
import jax
import jax.numpy as jnp
from jax import lax

C = 1024
B = 256
CLASSES = 1000
PIX = 28
STEPS = 2
IMG_DEV = 4
MUT_DEV = 4
SURV = 14
IMAGES = 2048
MUTANTS = 128
SURV_ALL = 224
CAP = 2


def draw_remaining_pictures(key, part):
    n_mut = MUTANTS // MUT_DEV
    n_test = SURV_ALL // SURV
    wanted = MUT_DEV * SURV
    pool_size = n_mut * CAP

    def one_group(group_key):
        key_a, key_b, key_c = jax.random.split(group_key, 3)
        perm = jax.random.permutation(key_a, pool_size)
        pool = perm // CAP
        position = jnp.arange(pool_size, dtype=jnp.int32)
        order_key = jnp.where(pool == pool[0], position - pool_size, position)
        ordered = pool[jnp.argsort(order_key, stable=True)][:wanted]
        ordered = ordered[jax.random.permutation(key_b, wanted)]
        within = jax.random.randint(key_c, (wanted,), 0, IMG_DEV)
        return (ordered * IMG_DEV + within).astype(jnp.int32)
    keys = jax.random.split(jax.random.fold_in(key, 11), n_mut * n_test)
    table = jax.vmap(one_group)(keys)
    table = table.reshape(n_mut, n_test, MUT_DEV, SURV)
    table = jnp.transpose(table, (0, 2, 1, 3))
    return table.reshape(MUTANTS, SURV_ALL).astype(jnp.int32)


def draw_input_activation(key, part):
    key_a = jax.random.fold_in(jax.random.fold_in(key, 23), 0)
    values = jax.random.normal(key_a, (IMAGES, PIX, C), jnp.float32)
    return jnp.clip(values, -6.0, 6.0).astype(jnp.bfloat16)


def draw_readout_matrix(key, part):
    key_a = jax.random.fold_in(jax.random.fold_in(key, 37), 0)
    values = jax.random.normal(key_a, (C, CLASSES), jnp.float32) * (1.0 / math.sqrt(C))
    return jnp.clip(values, -1.0, 1.0).astype(jnp.bfloat16)


def place_ends(result, rng, smallest, largest):
    spot = [jax.random.randint(jax.random.fold_in(rng, axis), (), 0, length) for axis, length in enumerate(result.shape)]
    longest = result.shape.index(max(result.shape))
    neighbour = spot[:longest] + [(spot[longest] + 1) % result.shape[longest]] + spot[longest + 1:]
    return result.at[tuple(spot)].set(smallest).at[tuple(neighbour)].set(largest)


def levels(stream_key, extent, cuts, least, largest):
    gain = 1.0
    for dim, shards_of in cuts:
        heights = jax.random.uniform(jax.random.fold_in(jax.random.fold_in(stream_key, 6), dim), (shards_of,), jnp.float32, least / len(cuts), largest / len(cuts))
        gain = gain * jnp.repeat(jnp.exp(heights), extent[dim] // shards_of).reshape((-1,) + (1,) * (len(extent) - 1 - dim))
    return gain


def gaussian(key, shape, spread, limit, cuts=(), held_as=jnp.bfloat16):
    values = jax.random.normal(key, shape, jnp.float32) * spread
    if len(cuts) > 0:
        values = levels(key, shape, cuts, -0.22, 0.18) * values
    return jnp.clip(values, min=-limit, max=limit).astype(held_as)


def setup_inputs(seed: int = 0) -> dict:
    key_list = jax.random.split(jax.random.key(seed), 10)
    return {
        "input_activation": draw_input_activation(jax.random.fold_in(key_list[9], 71), 0),
        "ground_truth_class": place_ends(jax.random.randint(key_list[1], (IMAGES,), 0, CLASSES), jax.random.fold_in(key_list[1], 1), 0, CLASSES - 1).astype(jnp.int32),
        "remaining_pictures": draw_remaining_pictures(jax.random.fold_in(key_list[9], 71), 0),
        "learned_narrowing_kernel": gaussian(key_list[3], (C, B), C ** -0.5, 0.1875),
        "learned_widening_kernel": gaussian(key_list[4], (B, C), B ** -0.5, 0.375),
        "narrowing_perturbation": gaussian(key_list[5], (MUTANTS, C, B), (4 * C) ** -0.5, 0.09375, ((0, 32), (1, 16))),
        "widening_perturbation": gaussian(key_list[6], (MUTANTS, B, C), (4 * B) ** -0.5, 0.1875, ((0, 32), (2, 16))),
        "perturbation_strength": jnp.clip(jnp.exp(math.log(2.0) - 2.0794415 * jax.random.uniform(key_list[7], (MUTANTS, STEPS), jnp.float32) ** levels(key_list[7], (MUTANTS, STEPS), ((0, 32),), -0.2, 0.2)), 0.25, 2.0),
        "readout_matrix": draw_readout_matrix(jax.random.fold_in(key_list[9], 71), 0),
    }


def evaluate(x_block, target_class_slice, mags, d_first, d_last, learned_narrowing_kernel, learned_widening_kernel, readout_matrix):
    rows = x_block.reshape(-1, x_block.shape[2])
    kills = []
    for step in range(STEPS):
        w_first = (learned_narrowing_kernel.astype(jnp.float32) + mags[step] * d_first.astype(jnp.float32)).astype(jnp.bfloat16)
        w_last = (learned_widening_kernel.astype(jnp.float32) + mags[step] * d_last.astype(jnp.float32)).astype(jnp.bfloat16)
        hidden = jnp.maximum(jnp.dot(rows, w_first, preferred_element_type=jnp.float32), 0.0).astype(jnp.bfloat16)
        out_rows = jnp.maximum(jnp.dot(hidden, w_last, preferred_element_type=jnp.float32) + rows.astype(jnp.float32), 0.0)
        pooled = jnp.mean(out_rows.reshape(x_block.shape), axis=1).astype(jnp.bfloat16)
        logits = jnp.dot(pooled, readout_matrix, preferred_element_type=jnp.float32)
        top = jnp.max(logits, axis=1, keepdims=True)
        total = top[:, 0] + jnp.log(jnp.sum(jnp.exp(logits - top), axis=1))
        column = jnp.arange(logits.shape[1], dtype=jnp.int32)
        selected_entries = jnp.sum(jnp.where(column[None, :] == target_class_slice[:, None], logits, 0.0), axis=1)
        kills.append(total - selected_entries)
    return jnp.stack(kills)


def reference(input_activation, ground_truth_class, remaining_pictures, learned_narrowing_kernel, learned_widening_kernel, narrowing_perturbation, widening_perturbation, perturbation_strength, readout_matrix):
    n_test = SURV_ALL // SURV
    shard = (jnp.arange(SURV_ALL, dtype=jnp.int32) // SURV).astype(jnp.int32)

    def one_mutant(variant_number):
        killing_tally = remaining_pictures[variant_number]
        whole = (((killing_tally // IMG_DEV) * n_test + shard) * IMG_DEV + killing_tally % IMG_DEV).astype(jnp.int32)
        x_block = jnp.take(input_activation, whole, axis=0)
        target_class_slice = jnp.take(ground_truth_class, whole)
        return evaluate(x_block, target_class_slice, perturbation_strength[variant_number], narrowing_perturbation[variant_number], widening_perturbation[variant_number], learned_narrowing_kernel, learned_widening_kernel, readout_matrix)

    return lax.map(one_mutant, jnp.arange(MUTANTS, dtype=jnp.int32))
```

```python
import jax
import jax.numpy as jnp
from jax import lax
from jax.experimental import pallas as pl
from jax.experimental.pallas import tpu as pltpu
from jax.sharding import Mesh, PartitionSpec as P

N_Y = 8
N_TEST = 16
IMG_DEV = 4
PIX = 28
SLOT = 32
SURV = 14
MUT_DEV = 4
STEPS = 2
C = 1024
B = 256
CHUNK = C // N_TEST
ROWS = SURV * SLOT


def build_weights(origin_ref, strength_ref, first_base_ref, last_base_ref, *refs):
    pieces = refs[:N_TEST]
    first_ref, last_ref = refs[N_TEST:]
    member = pl.program_id(0)
    for number in range(N_TEST):
        row = pl.multiple_of(origin_ref[number] * CHUNK, CHUNK)
        for kind, base_ref in enumerate((first_base_ref, last_base_ref)):
            base = base_ref[pl.ds(row, CHUNK), :].astype(jnp.float32)
            change = pieces[number][0, kind].astype(jnp.float32)
            for step in range(STEPS):
                value = (base + strength_ref[member, step] * change).astype(jnp.bfloat16)
                if kind == 0:
                    first_ref[0, pl.ds(row, CHUNK), step * B : (step + 1) * B] = value
                else:
                    last_ref[0, step, pl.ds(row, CHUNK), :] = value


def score(
    start_ref,
    images_ref,
    first_ref,
    last_ref,
    keep_low_ref,
    keep_high_ref,
    label_ref,
    readout_hbm_ref,
    out_ref,
    x_ref,
    pooled_ref,
    readout_ref,
    image_sem,
    readout_sem,
):
    member = pl.program_id(0)

    @pl.when(member == 0)
    def _():
        for variant in range(MUT_DEV):
            for entry in range(SURV):
                start = pl.multiple_of(start_ref[variant * SURV + entry], 8)
                pltpu.make_async_copy(
                    images_ref.at[pl.ds(start, SLOT)],
                    x_ref.at[variant, pl.ds(entry * SLOT, SLOT)],
                    image_sem.at[variant],
                ).start()
        pltpu.make_async_copy(readout_hbm_ref, readout_ref, readout_sem).start()
        pooled_ref[...] = jnp.zeros_like(pooled_ref)

    pltpu.make_async_copy(
        images_ref.at[pl.ds(0, ROWS)], x_ref.at[member], image_sem.at[member]
    ).wait()
    rows = x_ref[member]
    hidden = jnp.maximum(
        jnp.dot(rows, first_ref[0], preferred_element_type=jnp.float32), 0.0
    ).astype(jnp.bfloat16)
    for step in range(STEPS):
        expanded = lax.dot_general(
            hidden[:, step * B : (step + 1) * B],
            last_ref[0, step],
            (((1,), (1,)), ((), ())),
            preferred_element_type=jnp.float32,
        )
        out_rows = jnp.maximum(expanded + rows.astype(jnp.float32), 0.0)
        tiles = out_rows.reshape(SURV, SLOT // 8, 8, C)
        total = (
            tiles[:, 0] * keep_low_ref[0][:, :, :1]
            + tiles[:, 1]
            + tiles[:, 2]
            + tiles[:, 3] * keep_high_ref[0][:, :, :1]
        )
        pooled = (jnp.sum(total, axis=1) / PIX).astype(jnp.bfloat16)
        pooled_ref[member * STEPS + step, :SURV, :] = pooled

    @pl.when(member == MUT_DEV - 1)
    def _():
        pltpu.make_async_copy(readout_hbm_ref, readout_ref, readout_sem).wait()
        logits = jnp.dot(
            pooled_ref[...].reshape(MUT_DEV * STEPS * 16, C),
            readout_ref[...],
            preferred_element_type=jnp.float32,
        )
        top = jnp.max(logits, axis=1, keepdims=True)
        total = top + jnp.log(jnp.sum(jnp.exp(logits - top), axis=1, keepdims=True))
        column = lax.broadcasted_iota(jnp.int32, logits.shape, 1)
        chosen = jnp.sum(
            jnp.where(column == label_ref[...], logits, 0.0), axis=1, keepdims=True
        )
        kill = total - chosen
        shape = (MUT_DEV * STEPS * 16, 128)
        diagonal = lax.broadcasted_iota(jnp.int32, shape, 1) == (
            lax.broadcasted_iota(jnp.int32, shape, 0) % 16
        )
        spread = jnp.where(diagonal, jnp.broadcast_to(kill, shape), 0.0)
        lined = jnp.sum(spread.reshape(MUT_DEV * STEPS, 16, 128), axis=1)
        for variant in range(MUT_DEV):
            out_ref[variant] = lined[variant * STEPS : (variant + 1) * STEPS, :SURV]


def on_device(
    input_activation,
    ground_truth_class,
    remaining_pictures,
    learned_narrowing_kernel,
    learned_widening_kernel,
    narrowing_perturbation,
    widening_perturbation,
    perturbation_strength,
    readout_matrix,
):
    swap = [(0, 1), (1, 0)]
    up = [(i, (i + 1) % N_Y) for i in range(N_Y)]
    down = [(i, (i - 1) % N_Y) for i in range(N_Y)]
    my_xl = lax.axis_index("xl")
    my_xh = lax.axis_index("xh")
    my_y = lax.axis_index("y")

    own_rows = input_activation.reshape(IMG_DEV * PIX, C)
    partner_rows = lax.ppermute(own_rows, "xl", swap)
    images = lax.all_gather(
        jnp.concatenate([own_rows, partner_rows]), ("z", "core"), axis=0, tiled=True
    )

    message = jnp.stack(
        [narrowing_perturbation, jnp.transpose(widening_perturbation, (0, 2, 1))], axis=1
    )
    other = lax.ppermute(message, "xh", swap)
    pieces, origins = [], []
    for plane, seed in ((my_xh, message), (1 - my_xh, other)):
        pieces.append(seed)
        origins.append(plane * N_Y + my_y)
        going_up = going_down = seed
        for hop in range(1, 5):
            going_up = lax.ppermute(going_up, "y", up)
            pieces.append(going_up)
            origins.append(plane * N_Y + (my_y - hop) % N_Y)
            if hop < 4:
                going_down = lax.ppermute(going_down, "y", down)
                pieces.append(going_down)
                origins.append(plane * N_Y + (my_y + hop) % N_Y)
    origin = jnp.stack(origins).astype(jnp.int32)

    smem = pl.BlockSpec(memory_space=pltpu.SMEM)
    hbm = pl.BlockSpec(memory_space=pl.ANY)
    piece_spec = pl.BlockSpec((1, 2, CHUNK, B), lambda m: (m, 0, 0, 0))
    first_spec = pl.BlockSpec((1, C, STEPS * B), lambda m: (m, 0, 0))
    last_spec = pl.BlockSpec((1, STEPS, C, B), lambda m: (m, 0, 0, 0))
    base_spec = pl.BlockSpec((C, B), lambda m: (0, 0))
    first_all, last_all = pl.pallas_call(
        build_weights,
        grid=(MUT_DEV,),
        in_specs=[smem, smem, base_spec, base_spec] + [piece_spec] * N_TEST,
        out_specs=[first_spec, last_spec],
        out_shape=[
            jax.ShapeDtypeStruct((MUT_DEV, C, STEPS * B), jnp.bfloat16),
            jax.ShapeDtypeStruct((MUT_DEV, STEPS, C, B), jnp.bfloat16),
        ],
        compiler_params=pltpu.CompilerParams(vmem_limit_bytes=40 * 2**20),
    )(
        origin,
        perturbation_strength,
        learned_narrowing_kernel,
        learned_widening_kernel.T,
        *pieces,
    )

    wanted = remaining_pictures.reshape(-1)
    holder = wanted // IMG_DEV
    within = wanted % IMG_DEV
    shard = my_xh * N_Y + my_y
    label = jnp.take(ground_truth_class, (holder * N_TEST + shard) * IMG_DEV + within)
    slot = (holder // 16 != my_xl).astype(jnp.int32)
    start = (
        ((holder % 16) * 2 + slot) * (IMG_DEV * PIX) + (within // 2) * (2 * PIX) + (within % 2) * 24
    )
    odd = (within % 2).reshape(MUT_DEV, SURV, 1, 1)
    sublane = jnp.arange(8, dtype=jnp.int32).reshape(1, 1, 8, 1)
    keep_shape = (MUT_DEV, SURV, 8, 128)
    keep_low = jnp.broadcast_to(
        jnp.where((odd == 0) | (sublane >= 4), 1.0, 0.0), keep_shape
    ).astype(jnp.float32)
    keep_high = jnp.broadcast_to(
        jnp.where((odd == 1) | (sublane < 4), 1.0, 0.0), keep_shape
    ).astype(jnp.float32)
    label_rows = jnp.broadcast_to(
        jnp.pad(label.reshape(MUT_DEV, 1, SURV), ((0, 0), (0, 0), (0, 2))), (MUT_DEV, STEPS, 16)
    ).reshape(MUT_DEV * STEPS * 16, 1)

    keep_spec = pl.BlockSpec((1, SURV, 8, 128), lambda m: (m, 0, 0, 0))
    return pl.pallas_call(
        score,
        grid=(MUT_DEV,),
        in_specs=[
            smem,
            hbm,
            first_spec,
            last_spec,
            keep_spec,
            keep_spec,
            pl.BlockSpec((MUT_DEV * STEPS * 16, 1), lambda m: (0, 0)),
            hbm,
        ],
        out_specs=pl.BlockSpec((MUT_DEV, STEPS, SURV), lambda m: (0, 0, 0)),
        out_shape=jax.ShapeDtypeStruct((MUT_DEV, STEPS, SURV), jnp.float32),
        scratch_shapes=[
            pltpu.VMEM((MUT_DEV, ROWS, C), jnp.bfloat16),
            pltpu.VMEM((MUT_DEV * STEPS, 16, C), jnp.bfloat16),
            pltpu.VMEM((C, readout_matrix.shape[1]), jnp.bfloat16),
            pltpu.SemaphoreType.DMA((MUT_DEV,)),
            pltpu.SemaphoreType.DMA,
        ],
        compiler_params=pltpu.CompilerParams(vmem_limit_bytes=48 * 2**20),
    )(start, images, first_all, last_all, keep_low, keep_high, label_rows, readout_matrix)


def solution(mesh):
    fine = Mesh(mesh.devices.reshape(2, 8, 2, 2, N_Y), ("xl", "z", "core", "xh", "y"))
    mut = ("xl", "z", "core")
    test = ("xh", "y")
    return jax.shard_map(
        on_device,
        mesh=fine,
        in_specs=(
            P(mut + test, None, None),
            P(),
            P(mut, test),
            P(),
            P(),
            P(mut, test, None),
            P(mut, None, test),
            P(mut, None),
            P(),
        ),
        out_specs=P(mut, None, test),
        check_vma=False,
    )
```

```python
import jax
import jax.numpy as jnp
from jax import lax
from jax.experimental import pallas as pl
from jax.experimental.pallas import tpu as pltpu
from jax.sharding import Mesh, PartitionSpec as P

N_Y = 8
N_TEST = 16
IMG_DEV = 4
PIX = 28
SLOT = 32
SURV = 14
MUT_DEV = 4
STEPS = 2
C = 1024
B = 256
CHUNK = C // N_TEST
ROWS = SURV * SLOT
OFFSETS = (0, -1, -2, -3, 1, 2, 3, 4)


def in_hbm(value):
    return pltpu.with_memory_space_constraint(value, pltpu.HBM)


def build_weights(strength_ref, first_base_ref, last_base_ref, *refs):
    whole = refs[: N_TEST - 2]
    halves = refs[N_TEST - 2 : N_TEST + 2]
    first_ref, last_ref = refs[N_TEST + 2 :]
    member = pl.program_id(0)
    my_xh = lax.axis_index("xh")
    my_y = lax.axis_index("y")
    for number in range(N_TEST):
        plane = my_xh if number % 2 == 0 else 1 - my_xh
        origin = plane * N_Y + (my_y + OFFSETS[number // 2]) % N_Y
        row = pl.multiple_of(origin * CHUNK, CHUNK)
        for kind, base_ref in enumerate((first_base_ref, last_base_ref)):
            base = base_ref[pl.ds(row, CHUNK), :].astype(jnp.float32)
            if number < N_TEST - 2:
                change = whole[number][0, kind]
            else:
                low, high = halves[(number % 2) * 2 : (number % 2) * 2 + 2]
                change = jnp.where(member < MUT_DEV // 2, low[0, kind], high[0, kind])
            change = change.astype(jnp.float32)
            for step in range(STEPS):
                value = (base + strength_ref[step, member] * change).astype(jnp.bfloat16)
                if kind == 0:
                    first_ref[0, pl.ds(row, CHUNK), step * B : (step + 1) * B] = value
                else:
                    last_ref[0, step, pl.ds(row, CHUNK), :] = value


def score(
    wanted_ref,
    class_ref,
    images_ref,
    first_ref,
    last_ref,
    readout_hbm_ref,
    out_ref,
    x_ref,
    pooled_ref,
    keep_ref,
    label_ref,
    readout_ref,
    image_sem,
    readout_sem,
):
    member = pl.program_id(0)

    @pl.when(member == 0)
    def _():
        my_xl = lax.axis_index("xl")
        shard = lax.axis_index("xh") * N_Y + lax.axis_index("y")
        sublane = lax.broadcasted_iota(jnp.int32, (8, 128), 0)
        for variant in range(MUT_DEV):
            for entry in range(SURV):
                wanted = wanted_ref[variant, entry]
                holder = wanted // IMG_DEV
                within = wanted % IMG_DEV
                slot = jnp.where(holder // 16 != my_xl, 1, 0)
                start = (
                    ((holder % 16) * 2 + slot) * (IMG_DEV * PIX)
                    + (within // 2) * (2 * PIX)
                    + (within % 2) * 24
                )
                pltpu.make_async_copy(
                    images_ref.at[pl.ds(pl.multiple_of(start, 8), SLOT)],
                    x_ref.at[variant, pl.ds(entry * SLOT, SLOT)],
                    image_sem.at[variant],
                ).start()
        pltpu.make_async_copy(readout_hbm_ref, readout_ref, readout_sem).start()
        pooled_ref[...] = jnp.zeros_like(pooled_ref)
        label_ref[...] = jnp.zeros_like(label_ref)
        for variant in range(MUT_DEV):
            for entry in range(SURV):
                wanted = wanted_ref[variant, entry]
                holder = wanted // IMG_DEV
                within = wanted % IMG_DEV
                odd = within % 2
                keep_ref[variant, 0, entry] = jnp.where(sublane >= odd * 4, 1.0, 0.0)
                keep_ref[variant, 1, entry] = jnp.where(sublane < 4 + odd * 4, 1.0, 0.0)
                label = class_ref[(holder * N_TEST + shard) * IMG_DEV + within]
                for step in range(STEPS):
                    row = (variant * STEPS + step) * 16 + entry
                    label_ref[row : row + 1, :] = jnp.full((1, 128), label, jnp.int32)

    pltpu.make_async_copy(
        images_ref.at[pl.ds(0, ROWS)], x_ref.at[member], image_sem.at[member]
    ).wait()
    rows = x_ref[member]
    hidden = jnp.maximum(
        jnp.dot(rows, first_ref[0], preferred_element_type=jnp.float32), 0.0
    ).astype(jnp.bfloat16)
    for step in range(STEPS):
        expanded = lax.dot_general(
            hidden[:, step * B : (step + 1) * B],
            last_ref[0, step],
            (((1,), (1,)), ((), ())),
            preferred_element_type=jnp.float32,
        )
        out_rows = jnp.maximum(expanded + rows.astype(jnp.float32), 0.0)
        tiles = out_rows.reshape(SURV, SLOT // 8, 8, C)
        total = (
            tiles[:, 0] * keep_ref[member, 0][:, :, :1]
            + tiles[:, 1]
            + tiles[:, 2]
            + tiles[:, 3] * keep_ref[member, 1][:, :, :1]
        )
        pooled = (jnp.sum(total, axis=1) / PIX).astype(jnp.bfloat16)
        pooled_ref[member * STEPS + step, :SURV, :] = pooled

    @pl.when(member == MUT_DEV - 1)
    def _():
        pltpu.make_async_copy(readout_hbm_ref, readout_ref, readout_sem).wait()
        logits = lax.dot_general(
            pooled_ref[...].reshape(MUT_DEV * STEPS * 16, C),
            readout_ref[...],
            (((1,), (1,)), ((), ())),
            preferred_element_type=jnp.float32,
        )
        top = jnp.max(logits, axis=1, keepdims=True)
        total = top + jnp.log(jnp.sum(jnp.exp(logits - top), axis=1, keepdims=True))
        column = lax.broadcasted_iota(jnp.int32, logits.shape, 1)
        chosen = jnp.sum(
            jnp.where(column == label_ref[:, :1], logits, 0.0), axis=1, keepdims=True
        )
        kill = total - chosen
        shape = (MUT_DEV * STEPS * 16, 128)
        diagonal = lax.broadcasted_iota(jnp.int32, shape, 1) == (
            lax.broadcasted_iota(jnp.int32, shape, 0) % 16
        )
        spread = jnp.where(diagonal, jnp.broadcast_to(kill, shape), 0.0)
        lined = jnp.sum(spread.reshape(MUT_DEV * STEPS, 16, 128), axis=1)
        for variant in range(MUT_DEV):
            out_ref[variant] = lined[variant * STEPS : (variant + 1) * STEPS, :SURV]


def on_device(
    input_activation,
    ground_truth_class,
    remaining_pictures,
    learned_narrowing_kernel,
    learned_widening_kernel,
    narrowing_perturbation,
    widening_perturbation,
    perturbation_strength,
    readout_matrix,
):
    swap = [(0, 1), (1, 0)]
    up = [(i, (i + 1) % N_Y) for i in range(N_Y)]
    down = [(i, (i - 1) % N_Y) for i in range(N_Y)]

    own_rows = input_activation.reshape(IMG_DEV * PIX, C)
    message = jnp.stack(
        [narrowing_perturbation, jnp.transpose(widening_perturbation, (0, 2, 1))], axis=1
    )
    own_rows, message = lax.optimization_barrier((own_rows, message))
    partner_rows = lax.ppermute(own_rows, "xl", swap)
    first_up = lax.ppermute(message, "y", up)
    partner_rows, first_up = lax.optimization_barrier((partner_rows, first_up))
    images = lax.all_gather(
        jnp.concatenate([own_rows, partner_rows]), ("z", "core"), axis=0, tiled=True
    )

    other = lax.ppermute(message, "xh", swap)
    flows = []
    for seed in (message, other):
        rising = [first_up if seed is message else lax.ppermute(seed, "y", up)]
        falling = [lax.ppermute(seed, "y", down)]
        for _ in range(2):
            rising.append(lax.ppermute(rising[-1], "y", up))
            falling.append(lax.ppermute(falling[-1], "y", down))
        half = MUT_DEV // 2
        low = lax.ppermute(rising[-1][:half], "y", up)
        high = lax.ppermute(falling[-1][half:], "y", down)
        flows.append(([seed] + rising + falling, [low, high]))
    pieces = [flows[number % 2][0][number // 2] for number in range(N_TEST - 2)]
    pieces += flows[0][1] + flows[1][1]

    smem = pl.BlockSpec(memory_space=pltpu.SMEM)
    hbm = pl.BlockSpec(memory_space=pl.ANY)
    piece = (1, 2, CHUNK, B)
    whole_spec = pl.BlockSpec(piece, lambda m: (m, 0, 0, 0))
    low_spec = pl.BlockSpec(piece, lambda m: (jnp.minimum(m, MUT_DEV // 2 - 1), 0, 0, 0))
    high_spec = pl.BlockSpec(piece, lambda m: (jnp.maximum(m - MUT_DEV // 2, 0), 0, 0, 0))
    first_spec = pl.BlockSpec((1, C, STEPS * B), lambda m: (m, 0, 0))
    last_spec = pl.BlockSpec((1, STEPS, C, B), lambda m: (m, 0, 0, 0))
    base_spec = pl.BlockSpec((C, B), lambda m: (0, 0))
    first_all, last_all = pl.pallas_call(
        build_weights,
        grid=(MUT_DEV,),
        in_specs=[smem, base_spec, base_spec]
        + [whole_spec] * (N_TEST - 2)
        + [low_spec, high_spec] * 2,
        out_specs=[first_spec, last_spec],
        out_shape=[
            pltpu.HBM((MUT_DEV, C, STEPS * B), jnp.bfloat16),
            pltpu.HBM((MUT_DEV, STEPS, C, B), jnp.bfloat16),
        ],
        compiler_params=pltpu.CompilerParams(vmem_limit_bytes=14 * 2**20),
    )(
        perturbation_strength.T,
        in_hbm(learned_narrowing_kernel),
        learned_widening_kernel.T,
        *[in_hbm(value) for value in pieces],
    )

    return pl.pallas_call(
        score,
        grid=(MUT_DEV,),
        in_specs=[smem, smem, hbm, first_spec, last_spec, hbm],
        out_specs=pl.BlockSpec((MUT_DEV, STEPS, SURV), lambda m: (0, 0, 0)),
        out_shape=jax.ShapeDtypeStruct((MUT_DEV, STEPS, SURV), jnp.float32),
        scratch_shapes=[
            pltpu.VMEM((MUT_DEV, ROWS, C), jnp.bfloat16),
            pltpu.VMEM((MUT_DEV * STEPS, 16, C), jnp.bfloat16),
            pltpu.VMEM((MUT_DEV, 2, SURV, 8, 128), jnp.float32),
            pltpu.VMEM((MUT_DEV * STEPS * 16, 128), jnp.int32),
            pltpu.VMEM((readout_matrix.shape[1], C), jnp.bfloat16),
            pltpu.SemaphoreType.DMA((MUT_DEV,)),
            pltpu.SemaphoreType.DMA,
        ],
        compiler_params=pltpu.CompilerParams(vmem_limit_bytes=26 * 2**20),
    )(
        remaining_pictures,
        ground_truth_class,
        in_hbm(images),
        in_hbm(first_all),
        in_hbm(last_all),
        in_hbm(readout_matrix.T),
    )


def solution(mesh):
    fine = Mesh(mesh.devices.reshape(2, 8, 2, 2, N_Y), ("xl", "z", "core", "xh", "y"))
    mut = ("xl", "z", "core")
    test = ("xh", "y")
    return jax.shard_map(
        on_device,
        mesh=fine,
        in_specs=(
            P(mut + test, None, None),
            P(),
            P(mut, test),
            P(),
            P(),
            P(mut, test, None),
            P(mut, None, test),
            P(mut, None),
            P(),
        ),
        out_specs=P(mut, None, test),
        check_vma=False,
    )
```

```python
import jax
import jax.numpy as jnp
from jax import lax
from jax.experimental import pallas as pl
from jax.experimental.pallas import tpu as pltpu
from jax.sharding import Mesh, PartitionSpec as P

N_Y = 8
N_TEST = 16
IMG_DEV = 4
PIX = 28
SLOT = 32
SURV = 14
MUT_DEV = 4
STEPS = 2
C = 1024
B = 256
CHUNK = C // N_TEST
ROWS = SURV * SLOT
OFFSETS = (0, -1, -2, -3, 1, 2, 3, 4)


def in_hbm(value):
    return pltpu.with_memory_space_constraint(value, pltpu.HBM)


def in_vmem(value):
    return pltpu.with_memory_space_constraint(value, pltpu.VMEM)


def score(*refs):
    wanted_ref, class_ref, strength_ref, images_ref, readout_hbm_ref = refs[:5]
    base_ref = refs[5]
    pieces = refs[6 : 6 + N_TEST]
    out_ref = refs[6 + N_TEST]
    x_ref, pooled_ref, keep_ref, label_ref, readout_ref = refs[7 + N_TEST : 12 + N_TEST]
    first_refs = refs[12 + N_TEST : 14 + N_TEST]
    last_refs = refs[14 + N_TEST : 16 + N_TEST]
    image_sem, readout_sem = refs[16 + N_TEST :]
    my_xl = lax.axis_index("xl")
    my_xh = lax.axis_index("xh")
    my_y = lax.axis_index("y")
    shard = my_xh * N_Y + my_y

    for variant in range(MUT_DEV):
        for entry in range(SURV):
            wanted = wanted_ref[variant, entry]
            holder = wanted // IMG_DEV
            within = wanted % IMG_DEV
            slot = jnp.where(holder // 16 != my_xl, 1, 0)
            start = (
                ((holder % 16) * 2 + slot) * (IMG_DEV * PIX)
                + (within // 2) * (2 * PIX)
                + (within % 2) * 24
            )
            pltpu.make_async_copy(
                images_ref.at[pl.ds(pl.multiple_of(start, 8), SLOT)],
                x_ref.at[variant, pl.ds(entry * SLOT, SLOT)],
                image_sem.at[variant],
            ).start()
    pltpu.make_async_copy(readout_hbm_ref, readout_ref, readout_sem).start()

    rows_of = []
    for number in range(N_TEST):
        plane = my_xh if number % 2 == 0 else 1 - my_xh
        origin = plane * N_Y + (my_y + OFFSETS[number // 2] + N_Y) % N_Y
        rows_of.append(pl.multiple_of(origin * CHUNK, CHUNK))

    def build(member):
        for number in range(N_TEST):
            row = rows_of[number]
            for kind in range(2):
                base = base_ref[kind, pl.ds(row, CHUNK), :].astype(jnp.float32)
                change = pieces[number][member, kind].astype(jnp.float32)
                for step in range(STEPS):
                    value = (base + strength_ref[step, member] * change).astype(jnp.bfloat16)
                    if kind == 0:
                        first_refs[member % 2][pl.ds(row, CHUNK), step * B : (step + 1) * B] = value
                    else:
                        last_refs[member % 2][step, pl.ds(row, CHUNK), :] = value

    build(0)
    pooled_ref[...] = jnp.zeros_like(pooled_ref)
    label_ref[...] = jnp.zeros_like(label_ref)
    sublane = lax.broadcasted_iota(jnp.int32, (8, B), 0)
    for variant in range(MUT_DEV):
        for entry in range(SURV):
            wanted = wanted_ref[variant, entry]
            within = wanted % IMG_DEV
            odd = within % 2
            keep_ref[variant, 0, entry] = jnp.where(sublane >= odd * 4, 1.0, 0.0)
            keep_ref[variant, 1, entry] = jnp.where(sublane < 4 + odd * 4, 1.0, 0.0)
            label = class_ref[((wanted // IMG_DEV) * N_TEST + shard) * IMG_DEV + within]
            for step in range(STEPS):
                row = (variant * STEPS + step) * 16 + entry
                label_ref[row : row + 1, :] = jnp.full((1, 128), label, jnp.int32)

    for member in range(MUT_DEV):
        pltpu.make_async_copy(
            images_ref.at[pl.ds(0, ROWS)], x_ref.at[member], image_sem.at[member]
        ).wait()
        if member + 1 < MUT_DEV:
            build(member + 1)
        for step in range(STEPS):
            hidden = jnp.maximum(
                jnp.dot(
                    x_ref[member],
                    first_refs[member % 2][:, step * B : (step + 1) * B],
                    preferred_element_type=jnp.float32,
                ),
                0.0,
            ).astype(jnp.bfloat16)
            for part in range(C // B):
                columns = slice(part * B, (part + 1) * B)
                expanded = lax.dot_general(
                    hidden,
                    last_refs[member % 2][step, columns, :],
                    (((1,), (1,)), ((), ())),
                    preferred_element_type=jnp.float32,
                )
                out_rows = jnp.maximum(expanded + x_ref[member, :, columns].astype(jnp.float32), 0.0)
                tiles = out_rows.reshape(SURV, SLOT // 8, 8, B)
                total = (
                    tiles[:, 0] * keep_ref[member, 0]
                    + tiles[:, 1]
                    + tiles[:, 2]
                    + tiles[:, 3] * keep_ref[member, 1]
                )
                pooled = (jnp.sum(total, axis=1) / PIX).astype(jnp.bfloat16)
                pooled_ref[member * STEPS + step, :SURV, columns] = pooled

    pltpu.make_async_copy(readout_hbm_ref, readout_ref, readout_sem).wait()
    logits = lax.dot_general(
        pooled_ref[...].reshape(MUT_DEV * STEPS * 16, C),
        readout_ref[...],
        (((1,), (1,)), ((), ())),
        preferred_element_type=jnp.float32,
    )
    top = jnp.max(logits, axis=1, keepdims=True)
    total = top + jnp.log(jnp.sum(jnp.exp(logits - top), axis=1, keepdims=True))
    column = lax.broadcasted_iota(jnp.int32, logits.shape, 1)
    chosen = jnp.sum(jnp.where(column == label_ref[:, :1], logits, 0.0), axis=1, keepdims=True)
    kill = total - chosen
    shape = (MUT_DEV * STEPS * 16, 128)
    diagonal = lax.broadcasted_iota(jnp.int32, shape, 1) == (
        lax.broadcasted_iota(jnp.int32, shape, 0) % 16
    )
    spread = jnp.where(diagonal, jnp.broadcast_to(kill, shape), 0.0)
    lined = jnp.sum(spread.reshape(MUT_DEV * STEPS, 16, 128), axis=1)
    for variant in range(MUT_DEV):
        out_ref[variant] = lined[variant * STEPS : (variant + 1) * STEPS, :SURV]


def on_device(
    input_activation,
    ground_truth_class,
    remaining_pictures,
    learned_narrowing_kernel,
    learned_widening_kernel,
    narrowing_perturbation,
    widening_perturbation,
    perturbation_strength,
    readout_matrix,
):
    swap = [(0, 1), (1, 0)]
    up = [(i, (i + 1) % N_Y) for i in range(N_Y)]
    down = [(i, (i - 1) % N_Y) for i in range(N_Y)]

    own_rows = input_activation.reshape(IMG_DEV * PIX, C)
    message = jnp.stack(
        [narrowing_perturbation, jnp.transpose(widening_perturbation, (0, 2, 1))], axis=1
    )
    own_rows, message = lax.optimization_barrier((own_rows, message))
    partner_rows = lax.ppermute(own_rows, "xl", swap)
    first_up = lax.ppermute(message, "y", up)
    partner_rows, first_up = lax.optimization_barrier((partner_rows, first_up))
    images = lax.all_gather(
        jnp.concatenate([own_rows, partner_rows]), ("z", "core"), axis=0, tiled=True
    )

    other = lax.ppermute(message, "xh", swap)
    flows = []
    for number, seed in enumerate((message, other)):
        rising = [first_up if number == 0 else lax.ppermute(seed, "y", up)]
        falling = [lax.ppermute(seed, "y", down)]
        for _ in range(2):
            rising.append(lax.ppermute(rising[-1], "y", up))
            falling.append(lax.ppermute(falling[-1], "y", down))
        if number == 0:
            farthest = lax.ppermute(rising[-1], "y", up)
        else:
            farthest = lax.ppermute(falling[-1], "y", down)
        flows.append([seed] + rising + falling + [farthest])
    pieces = [flows[number % 2][number // 2] for number in range(N_TEST)]

    bases = jnp.stack([learned_narrowing_kernel, learned_widening_kernel.T])
    smem = pl.BlockSpec(memory_space=pltpu.SMEM)
    vmem = pl.BlockSpec(memory_space=pltpu.VMEM)
    hbm = pl.BlockSpec(memory_space=pl.ANY)
    return pl.pallas_call(
        score,
        in_specs=[smem, smem, smem, hbm, hbm, vmem] + [vmem] * N_TEST,
        out_specs=vmem,
        out_shape=jax.ShapeDtypeStruct((MUT_DEV, STEPS, SURV), jnp.float32),
        scratch_shapes=[
            pltpu.VMEM((MUT_DEV, ROWS, C), jnp.bfloat16),
            pltpu.VMEM((MUT_DEV * STEPS, 16, C), jnp.bfloat16),
            pltpu.VMEM((MUT_DEV, 2, SURV, 8, B), jnp.float32),
            pltpu.VMEM((MUT_DEV * STEPS * 16, 128), jnp.int32),
            pltpu.VMEM((readout_matrix.shape[1], C), jnp.bfloat16),
            pltpu.VMEM((C, STEPS * B), jnp.bfloat16),
            pltpu.VMEM((C, STEPS * B), jnp.bfloat16),
            pltpu.VMEM((STEPS, C, B), jnp.bfloat16),
            pltpu.VMEM((STEPS, C, B), jnp.bfloat16),
            pltpu.SemaphoreType.DMA((MUT_DEV,)),
            pltpu.SemaphoreType.DMA,
        ],
        compiler_params=pltpu.CompilerParams(vmem_limit_bytes=24 * 2**20),
    )(
        remaining_pictures,
        ground_truth_class,
        perturbation_strength.T,
        in_hbm(images),
        in_hbm(readout_matrix.T),
        in_vmem(bases),
        *[in_vmem(value) for value in pieces],
    )


def solution(mesh):
    fine = Mesh(mesh.devices.reshape(2, 8, 2, 2, N_Y), ("xl", "z", "core", "xh", "y"))
    mut = ("xl", "z", "core")
    test = ("xh", "y")
    return jax.shard_map(
        on_device,
        mesh=fine,
        in_specs=(
            P(mut + test, None, None),
            P(),
            P(mut, test),
            P(),
            P(),
            P(mut, test, None),
            P(mut, None, test),
            P(mut, None),
            P(),
        ),
        out_specs=P(mut, None, test),
        check_vma=False,
    )
```

```python
import jax
import jax.numpy as jnp
from jax import lax
from jax.experimental import pallas as pl
from jax.experimental.pallas import tpu as pltpu
from jax.sharding import Mesh, PartitionSpec as P

N_Y = 8
N_TEST = 16
IMG_DEV = 4
PIX = 28
SLOT = 32
SURV = 14
MUT_DEV = 4
STEPS = 2
C = 1024
B = 256
CHUNK = C // N_TEST
ROWS = SURV * SLOT
OFFSETS = (0, -1, -2, -3, 1, 2, 3, 4)


def in_hbm(value):
    return pltpu.with_memory_space_constraint(value, pltpu.HBM)


def in_vmem(value):
    return pltpu.with_memory_space_constraint(value, pltpu.VMEM)


def score(*refs):
    plan_ref, strength_ref, images_ref, readout_hbm_ref, base_ref = refs[:5]
    piece_hbm_refs = refs[5 : 5 + N_TEST]
    out_ref = refs[5 + N_TEST]
    x_ref, pooled_ref, keep_ref, label_ref, readout_ref = refs[6 + N_TEST : 11 + N_TEST]
    first_refs = refs[11 + N_TEST : 13 + N_TEST]
    last_refs = refs[13 + N_TEST : 15 + N_TEST]
    piece_refs = refs[15 + N_TEST : 15 + 2 * N_TEST]
    image_sem, readout_sem, piece_sem = refs[15 + 2 * N_TEST :]
    my_xh = lax.axis_index("xh")
    my_y = lax.axis_index("y")

    def fetch(variant):
        for entry in range(SURV):
            start = pl.multiple_of(plan_ref[0, variant * SURV + entry], 8)
            pltpu.make_async_copy(
                images_ref.at[pl.ds(start, SLOT)],
                x_ref.at[variant, pl.ds(entry * SLOT, SLOT)],
                image_sem.at[variant],
            ).start()

    piece_copies = []
    for number in range(N_TEST):
        copy = pltpu.make_async_copy(
            piece_hbm_refs[number], piece_refs[number], piece_sem.at[number]
        )
        copy.start()
        piece_copies.append(copy)
    for variant in range(MUT_DEV):
        fetch(variant)
    pltpu.make_async_copy(readout_hbm_ref, readout_ref, readout_sem).start()

    rows_of = []
    for number in range(N_TEST):
        plane = my_xh if number % 2 == 0 else 1 - my_xh
        origin = plane * N_Y + (my_y + OFFSETS[number // 2] + N_Y) % N_Y
        rows_of.append(pl.multiple_of(origin * CHUNK, CHUNK))

    def build(member):
        for number in range(N_TEST):
            row = rows_of[number]
            if member == 0:
                piece_copies[number].wait()
            for kind in range(2):
                base = base_ref[kind, pl.ds(row, CHUNK), :].astype(jnp.float32)
                change = piece_refs[number][member, kind].astype(jnp.float32)
                for step in range(STEPS):
                    value = (base + strength_ref[0, step * MUT_DEV + member] * change).astype(jnp.bfloat16)
                    if kind == 0:
                        first_refs[member % 2][pl.ds(row, CHUNK), step * B : (step + 1) * B] = value
                    else:
                        last_refs[member % 2][step, pl.ds(row, CHUNK), :] = value

    build(0)
    pooled_ref[...] = jnp.zeros_like(pooled_ref)
    label_ref[...] = jnp.zeros_like(label_ref)
    sublane = lax.broadcasted_iota(jnp.int32, (8, B), 0)
    for variant in range(MUT_DEV):
        for entry in range(SURV):
            odd = plan_ref[1, variant * SURV + entry]
            keep_ref[variant, 0, entry] = jnp.where(sublane >= odd * 4, 1.0, 0.0)
            keep_ref[variant, 1, entry] = jnp.where(sublane < 4 + odd * 4, 1.0, 0.0)
            label = plan_ref[2, variant * SURV + entry]
            for step in range(STEPS):
                row = (variant * STEPS + step) * 16 + entry
                label_ref[row : row + 1, :] = jnp.full((1, 128), label, jnp.int32)

    for member in range(MUT_DEV):
        pltpu.make_async_copy(
            images_ref.at[pl.ds(0, ROWS)], x_ref.at[member], image_sem.at[member]
        ).wait()
        if member + 1 < MUT_DEV:
            build(member + 1)
        for step in range(STEPS):
            hidden = jnp.maximum(
                jnp.dot(
                    x_ref[member],
                    first_refs[member % 2][:, step * B : (step + 1) * B],
                    preferred_element_type=jnp.float32,
                ),
                0.0,
            ).astype(jnp.bfloat16)
            for part in range(C // B):
                columns = slice(part * B, (part + 1) * B)
                expanded = lax.dot_general(
                    hidden,
                    last_refs[member % 2][step, columns, :],
                    (((1,), (1,)), ((), ())),
                    preferred_element_type=jnp.float32,
                )
                out_rows = jnp.maximum(expanded + x_ref[member, :, columns].astype(jnp.float32), 0.0)
                tiles = out_rows.reshape(SURV, SLOT // 8, 8, B)
                total = (
                    tiles[:, 0] * keep_ref[member, 0]
                    + tiles[:, 1]
                    + tiles[:, 2]
                    + tiles[:, 3] * keep_ref[member, 1]
                )
                pooled = (jnp.sum(total, axis=1) / PIX).astype(jnp.bfloat16)
                pooled_ref[member * STEPS + step, :SURV, columns] = pooled

    pltpu.make_async_copy(readout_hbm_ref, readout_ref, readout_sem).wait()
    logits = lax.dot_general(
        pooled_ref[...].reshape(MUT_DEV * STEPS * 16, C),
        readout_ref[...],
        (((1,), (1,)), ((), ())),
        preferred_element_type=jnp.float32,
    )
    top = jnp.max(logits, axis=1, keepdims=True)
    total = top + jnp.log(jnp.sum(jnp.exp(logits - top), axis=1, keepdims=True))
    column = lax.broadcasted_iota(jnp.int32, logits.shape, 1)
    chosen = jnp.sum(jnp.where(column == label_ref[:, :1], logits, 0.0), axis=1, keepdims=True)
    kill = total - chosen
    shape = (MUT_DEV * STEPS * 16, 128)
    diagonal = lax.broadcasted_iota(jnp.int32, shape, 1) == (
        lax.broadcasted_iota(jnp.int32, shape, 0) % 16
    )
    spread = jnp.where(diagonal, jnp.broadcast_to(kill, shape), 0.0)
    lined = jnp.sum(spread.reshape(MUT_DEV * STEPS, 16, 128), axis=1)
    for variant in range(MUT_DEV):
        out_ref[variant] = lined[variant * STEPS : (variant + 1) * STEPS, :SURV]


def on_device(
    input_activation,
    ground_truth_class,
    remaining_pictures,
    learned_narrowing_kernel,
    learned_widening_kernel,
    narrowing_perturbation,
    widening_perturbation,
    perturbation_strength,
    readout_matrix,
):
    swap = [(0, 1), (1, 0)]
    up = [(i, (i + 1) % N_Y) for i in range(N_Y)]
    down = [(i, (i - 1) % N_Y) for i in range(N_Y)]

    own_rows = input_activation.reshape(IMG_DEV * PIX, C)
    message = jnp.stack(
        [narrowing_perturbation, jnp.transpose(widening_perturbation, (0, 2, 1))], axis=1
    )
    partner_rows = lax.ppermute(own_rows, "xl", swap)
    images = lax.all_gather(
        jnp.concatenate([own_rows, partner_rows]), ("z", "core"), axis=0, tiled=True
    )

    other = lax.ppermute(message, "xh", swap)

    wanted = remaining_pictures.reshape(1, -1)
    holder = wanted // IMG_DEV
    within = wanted % IMG_DEV
    slot = (holder // 16 != lax.axis_index("xl")).astype(jnp.int32)
    start = (
        ((holder % 16) * 2 + slot) * (IMG_DEV * PIX) + (within // 2) * (2 * PIX) + (within % 2) * 24
    )
    shard = lax.axis_index("xh") * N_Y + lax.axis_index("y")
    label = jnp.take(ground_truth_class, (holder * N_TEST + shard) * IMG_DEV + within)
    plan = jnp.concatenate([start, within % 2, label])
    strength = jnp.pad(perturbation_strength.T.reshape(1, -1), ((0, 0), (0, 120)))
    bases = jnp.stack([learned_narrowing_kernel, learned_widening_kernel.T])
    other, plan, strength, bases = lax.optimization_barrier((other, plan, strength, bases))

    up_1 = lax.ppermute(message, "y", up)
    down_1 = lax.ppermute(message, "y", down)
    up_2 = lax.ppermute(up_1, "y", up)
    down_2 = lax.ppermute(down_1, "y", down)
    up_3 = lax.ppermute(up_2, "y", up)
    down_3 = lax.ppermute(down_2, "y", down)
    up_4 = lax.ppermute(up_3, "y", up)
    other_up_1 = lax.ppermute(up_1, "xh", swap)
    other_down_1 = lax.ppermute(down_1, "xh", swap)
    other_up_2 = lax.ppermute(up_2, "xh", swap)
    other_down_2 = lax.ppermute(down_2, "xh", swap)
    other_up_3 = lax.ppermute(other_up_2, "y", up)
    other_down_3 = lax.ppermute(other_down_2, "y", down)
    other_4 = lax.ppermute(other_down_3, "y", down)
    near = [message, up_1, up_2, up_3, down_1, down_2, down_3, up_4]
    far = [
        other,
        other_up_1,
        other_up_2,
        other_up_3,
        other_down_1,
        other_down_2,
        other_down_3,
        other_4,
    ]
    pieces = [(near, far)[number % 2][number // 2] for number in range(N_TEST)]

    smem = pl.BlockSpec(memory_space=pltpu.SMEM)
    vmem = pl.BlockSpec(memory_space=pltpu.VMEM)
    hbm = pl.BlockSpec(memory_space=pl.ANY)
    return pl.pallas_call(
        score,
        in_specs=[smem, smem, hbm, hbm, vmem] + [hbm] * N_TEST,
        out_specs=vmem,
        out_shape=jax.ShapeDtypeStruct((MUT_DEV, STEPS, SURV), jnp.float32),
        scratch_shapes=[
            pltpu.VMEM((MUT_DEV, ROWS, C), jnp.bfloat16),
            pltpu.VMEM((MUT_DEV * STEPS, 16, C), jnp.bfloat16),
            pltpu.VMEM((MUT_DEV, 2, SURV, 8, B), jnp.float32),
            pltpu.VMEM((MUT_DEV * STEPS * 16, 128), jnp.int32),
            pltpu.VMEM((readout_matrix.shape[1], C), jnp.bfloat16),
            pltpu.VMEM((C, STEPS * B), jnp.bfloat16),
            pltpu.VMEM((C, STEPS * B), jnp.bfloat16),
            pltpu.VMEM((STEPS, C, B), jnp.bfloat16),
            pltpu.VMEM((STEPS, C, B), jnp.bfloat16),
        ]
        + [pltpu.VMEM((MUT_DEV, 2, CHUNK, B), jnp.bfloat16)] * N_TEST
        + [
            pltpu.SemaphoreType.DMA((MUT_DEV,)),
            pltpu.SemaphoreType.DMA,
            pltpu.SemaphoreType.DMA((N_TEST,)),
        ],
        compiler_params=pltpu.CompilerParams(vmem_limit_bytes=30 * 2**20),
    )(
        plan,
        strength,
        in_hbm(images),
        in_hbm(readout_matrix.T),
        in_vmem(bases),
        *[in_hbm(value) for value in pieces],
    )


def solution(mesh):
    fine = Mesh(mesh.devices.reshape(2, 8, 2, 2, N_Y), ("xl", "z", "core", "xh", "y"))
    mut = ("xl", "z", "core")
    test = ("xh", "y")
    return jax.shard_map(
        on_device,
        mesh=fine,
        in_specs=(
            P(mut + test, None, None),
            P(),
            P(mut, test),
            P(),
            P(),
            P(mut, test, None),
            P(mut, None, test),
            P(mut, None),
            P(),
        ),
        out_specs=P(mut, None, test),
        check_vma=False,
    )
```

```python
import jax
import jax.numpy as jnp
from jax import lax
from jax.experimental import pallas as pl
from jax.experimental.pallas import tpu as pltpu
from jax.sharding import Mesh, PartitionSpec as P

N_Y = 8
N_TEST = 16
IMG_DEV = 4
PIX = 28
SLOT = 32
SURV = 14
MUT_DEV = 4
STEPS = 2
C = 1024
B = 256
CHUNK = C // N_TEST
ROWS = SURV * SLOT
OFFSETS = (0, -1, -2, -3, 1, 2, 3, 4)


def in_hbm(value):
    return pltpu.with_memory_space_constraint(value, pltpu.HBM)


def in_vmem(value):
    return pltpu.with_memory_space_constraint(value, pltpu.VMEM)


def score(*refs):
    plan_ref, strength_ref, images_ref, readout_hbm_ref, base_ref = refs[:5]
    piece_hbm_refs = refs[5 : 5 + N_TEST]
    out_ref = refs[5 + N_TEST]
    x_ref, pooled_ref, keep_ref, label_ref, readout_ref = refs[6 + N_TEST : 11 + N_TEST]
    first_refs = refs[11 + N_TEST : 13 + N_TEST]
    last_refs = refs[13 + N_TEST : 15 + N_TEST]
    piece_refs = refs[15 + N_TEST : 15 + 2 * N_TEST]
    image_sem, readout_sem, piece_sem = refs[15 + 2 * N_TEST :]
    my_xh = lax.axis_index("xh")
    my_y = lax.axis_index("y")

    def fetch(variant):
        for entry in range(SURV):
            start = pl.multiple_of(plan_ref[0, variant * SURV + entry], 8)
            pltpu.make_async_copy(
                images_ref.at[pl.ds(start, SLOT)],
                x_ref.at[variant, pl.ds(entry * SLOT, SLOT)],
                image_sem.at[variant],
            ).start()

    piece_copies = {}
    for variant in range(MUT_DEV):
        for number in range(N_TEST):
            copy = pltpu.make_async_copy(
                piece_hbm_refs[number].at[variant],
                piece_refs[number].at[variant],
                piece_sem.at[variant, number],
            )
            copy.start()
            piece_copies[variant, number] = copy
        fetch(variant)
    pltpu.make_async_copy(readout_hbm_ref, readout_ref, readout_sem).start()

    rows_of = []
    for number in range(N_TEST):
        plane = my_xh if number % 2 == 0 else 1 - my_xh
        origin = plane * N_Y + (my_y + OFFSETS[number // 2] + N_Y) % N_Y
        rows_of.append(pl.multiple_of(origin * CHUNK, CHUNK))

    def build(member):
        for number in range(N_TEST):
            row = rows_of[number]
            piece_copies[member, number].wait()
            for kind in range(2):
                base = base_ref[kind, pl.ds(row, CHUNK), :].astype(jnp.float32)
                change = piece_refs[number][member, kind].astype(jnp.float32)
                for step in range(STEPS):
                    value = (base + strength_ref[0, step * MUT_DEV + member] * change).astype(jnp.bfloat16)
                    if kind == 0:
                        first_refs[member % 2][pl.ds(row, CHUNK), step * B : (step + 1) * B] = value
                    else:
                        last_refs[member % 2][step, pl.ds(row, CHUNK), :] = value

    build(0)
    pooled_ref[...] = jnp.zeros_like(pooled_ref)
    label_ref[...] = jnp.zeros_like(label_ref)
    sublane = lax.broadcasted_iota(jnp.int32, (8, B), 0)
    for variant in range(MUT_DEV):
        for entry in range(SURV):
            odd = plan_ref[1, variant * SURV + entry]
            keep_ref[variant, 0, entry] = jnp.where(sublane >= odd * 4, 1.0, 0.0)
            keep_ref[variant, 1, entry] = jnp.where(sublane < 4 + odd * 4, 1.0, 0.0)
            label = plan_ref[2, variant * SURV + entry]
            for step in range(STEPS):
                row = (variant * STEPS + step) * 16 + entry
                label_ref[row : row + 1, :] = jnp.full((1, 128), label, jnp.int32)

    for member in range(MUT_DEV):
        pltpu.make_async_copy(
            images_ref.at[pl.ds(0, ROWS)], x_ref.at[member], image_sem.at[member]
        ).wait()
        if member + 1 < MUT_DEV:
            build(member + 1)
        both = jnp.maximum(
            jnp.dot(x_ref[member], first_refs[member % 2][...], preferred_element_type=jnp.float32),
            0.0,
        ).astype(jnp.bfloat16)
        for step in range(STEPS):
            hidden = both[:, step * B : (step + 1) * B]
            for part in range(C // B):
                columns = slice(part * B, (part + 1) * B)
                expanded = lax.dot_general(
                    hidden,
                    last_refs[member % 2][step, columns, :],
                    (((1,), (1,)), ((), ())),
                    preferred_element_type=jnp.float32,
                )
                out_rows = jnp.maximum(expanded + x_ref[member, :, columns].astype(jnp.float32), 0.0)
                tiles = out_rows.reshape(SURV, SLOT // 8, 8, B)
                total = (
                    tiles[:, 0] * keep_ref[member, 0]
                    + tiles[:, 1]
                    + tiles[:, 2]
                    + tiles[:, 3] * keep_ref[member, 1]
                )
                pooled = (jnp.sum(total, axis=1) / PIX).astype(jnp.bfloat16)
                pooled_ref[member * STEPS + step, :SURV, columns] = pooled

    pltpu.make_async_copy(readout_hbm_ref, readout_ref, readout_sem).wait()
    logits = lax.dot_general(
        pooled_ref[...].reshape(MUT_DEV * STEPS * 16, C),
        readout_ref[...],
        (((1,), (1,)), ((), ())),
        preferred_element_type=jnp.float32,
    )
    top = jnp.max(logits, axis=1, keepdims=True)
    total = top + jnp.log(jnp.sum(jnp.exp(logits - top), axis=1, keepdims=True))
    column = lax.broadcasted_iota(jnp.int32, logits.shape, 1)
    chosen = jnp.sum(jnp.where(column == label_ref[:, :1], logits, 0.0), axis=1, keepdims=True)
    kill = total - chosen
    shape = (MUT_DEV * STEPS * 16, 128)
    diagonal = lax.broadcasted_iota(jnp.int32, shape, 1) == (
        lax.broadcasted_iota(jnp.int32, shape, 0) % 16
    )
    spread = jnp.where(diagonal, jnp.broadcast_to(kill, shape), 0.0)
    lined = jnp.sum(spread.reshape(MUT_DEV * STEPS, 16, 128), axis=1)
    for variant in range(MUT_DEV):
        out_ref[variant] = lined[variant * STEPS : (variant + 1) * STEPS, :SURV]


def run_score(plan, strength, images, readout, bases, pieces):
    smem = pl.BlockSpec(memory_space=pltpu.SMEM)
    vmem = pl.BlockSpec(memory_space=pltpu.VMEM)
    hbm = pl.BlockSpec(memory_space=pl.ANY)
    return pl.pallas_call(
        score,
        in_specs=[smem, smem, hbm, hbm, vmem] + [hbm] * N_TEST,
        out_specs=vmem,
        out_shape=jax.ShapeDtypeStruct((MUT_DEV, STEPS, SURV), jnp.float32),
        scratch_shapes=[
            pltpu.VMEM((MUT_DEV, ROWS, C), jnp.bfloat16),
            pltpu.VMEM((MUT_DEV * STEPS, 16, C), jnp.bfloat16),
            pltpu.VMEM((MUT_DEV, 2, SURV, 8, B), jnp.float32),
            pltpu.VMEM((MUT_DEV * STEPS * 16, 128), jnp.int32),
            pltpu.VMEM((readout.shape[0], C), jnp.bfloat16),
            pltpu.VMEM((C, STEPS * B), jnp.bfloat16),
            pltpu.VMEM((C, STEPS * B), jnp.bfloat16),
            pltpu.VMEM((STEPS, C, B), jnp.bfloat16),
            pltpu.VMEM((STEPS, C, B), jnp.bfloat16),
        ]
        + [pltpu.VMEM((MUT_DEV, 2, CHUNK, B), jnp.bfloat16)] * N_TEST
        + [
            pltpu.SemaphoreType.DMA((MUT_DEV,)),
            pltpu.SemaphoreType.DMA,
            pltpu.SemaphoreType.DMA((MUT_DEV, N_TEST)),
        ],
        compiler_params=pltpu.CompilerParams(vmem_limit_bytes=30 * 2**20),
    )(
        plan,
        strength,
        in_hbm(images),
        in_hbm(readout),
        in_vmem(bases),
        *[in_hbm(value) for value in pieces],
    )


def on_device(
    input_activation,
    ground_truth_class,
    remaining_pictures,
    learned_narrowing_kernel,
    learned_widening_kernel,
    narrowing_perturbation,
    widening_perturbation,
    perturbation_strength,
    readout_matrix,
):
    swap = [(0, 1), (1, 0)]
    up = [(i, (i + 1) % N_Y) for i in range(N_Y)]
    down = [(i, (i - 1) % N_Y) for i in range(N_Y)]

    own_rows = input_activation.reshape(IMG_DEV * PIX, C)
    message = jnp.stack(
        [narrowing_perturbation, jnp.transpose(widening_perturbation, (0, 2, 1))], axis=1
    )
    partner_rows = lax.ppermute(own_rows, "xl", swap)
    first_up = lax.ppermute(message, "y", up)
    images = lax.all_gather(
        jnp.concatenate([own_rows, partner_rows]), ("z", "core"), axis=0, tiled=True
    )

    other = lax.ppermute(message, "xh", swap)

    wanted = remaining_pictures.reshape(1, -1)
    holder = wanted // IMG_DEV
    within = wanted % IMG_DEV
    slot = (holder // 16 != lax.axis_index("xl")).astype(jnp.int32)
    start = (
        ((holder % 16) * 2 + slot) * (IMG_DEV * PIX) + (within // 2) * (2 * PIX) + (within % 2) * 24
    )
    shard = lax.axis_index("xh") * N_Y + lax.axis_index("y")
    label = jnp.take(ground_truth_class, (holder * N_TEST + shard) * IMG_DEV + within)
    plan = jnp.concatenate([start, within % 2, label])
    strength = jnp.pad(perturbation_strength.T.reshape(1, -1), ((0, 0), (0, 120)))
    bases = jnp.stack([learned_narrowing_kernel, learned_widening_kernel.T])
    other, plan, strength, bases = lax.optimization_barrier((other, plan, strength, bases))

    flows = []
    for number, seed in enumerate((message, other)):
        rising = [first_up if number == 0 else lax.ppermute(seed, "y", up)]
        falling = [lax.ppermute(seed, "y", down)]
        for _ in range(2):
            rising.append(lax.ppermute(rising[-1], "y", up))
            falling.append(lax.ppermute(falling[-1], "y", down))
        if number == 0:
            farthest = lax.ppermute(rising[-1], "y", up)
        else:
            farthest = lax.ppermute(falling[-1], "y", down)
        flows.append([seed] + rising + falling + [farthest])
    pieces = [flows[number % 2][number // 2] for number in range(N_TEST)]

    return run_score(plan, strength, images, readout_matrix.T, bases, pieces)


def solution(mesh):
    fine = Mesh(mesh.devices.reshape(2, 8, 2, 2, N_Y), ("xl", "z", "core", "xh", "y"))
    mut = ("xl", "z", "core")
    test = ("xh", "y")
    return jax.shard_map(
        on_device,
        mesh=fine,
        in_specs=(
            P(mut + test, None, None),
            P(),
            P(mut, test),
            P(),
            P(),
            P(mut, test, None),
            P(mut, None, test),
            P(mut, None),
            P(),
        ),
        out_specs=P(mut, None, test),
        check_vma=False,
    )
```

```python
import jax
import jax.numpy as jnp
from jax import lax
from jax.experimental import pallas as pl
from jax.experimental.pallas import tpu as pltpu
from jax.sharding import Mesh, PartitionSpec as P

N_Y = 8
N_TEST = 16
IMG_DEV = 4
PIX = 28
SLOT = 32
SURV = 14
MUT_DEV = 4
STEPS = 2
C = 1024
B = 256
CHUNK = C // N_TEST
ROWS = SURV * SLOT
OFFSETS = (0, -1, -2, -3, 1, 2, 3, 4)


def in_hbm(value):
    return pltpu.with_memory_space_constraint(value, pltpu.HBM)


def in_vmem(value):
    return pltpu.with_memory_space_constraint(value, pltpu.VMEM)


def score(*refs):
    plan_ref, strength_ref, images_ref, readout_hbm_ref, base_ref = refs[:5]
    piece_hbm_refs = refs[5 : 5 + N_TEST]
    out_ref = refs[5 + N_TEST]
    x_ref, pooled_ref, keep_ref, label_ref, readout_ref = refs[6 + N_TEST : 11 + N_TEST]
    first_refs = refs[11 + N_TEST : 13 + N_TEST]
    last_refs = refs[13 + N_TEST : 15 + N_TEST]
    piece_refs = refs[15 + N_TEST : 15 + 2 * N_TEST]
    image_sem, readout_sem, piece_sem = refs[15 + 2 * N_TEST :]
    my_xh = lax.axis_index("xh")
    my_y = lax.axis_index("y")

    def fetch(variant):
        for entry in range(SURV):
            start = pl.multiple_of(plan_ref[0, variant * SURV + entry], 8)
            pltpu.make_async_copy(
                images_ref.at[pl.ds(start, SLOT)],
                x_ref.at[variant, pl.ds(entry * SLOT, SLOT)],
                image_sem.at[variant],
            ).start()

    piece_copies = {}
    for variant in range(MUT_DEV):
        for number in range(N_TEST):
            copy = pltpu.make_async_copy(
                piece_hbm_refs[number].at[variant],
                piece_refs[number].at[variant],
                piece_sem.at[variant, number],
            )
            copy.start()
            piece_copies[variant, number] = copy
        fetch(variant)
    pltpu.make_async_copy(readout_hbm_ref, readout_ref, readout_sem).start()

    rows_of = []
    for number in range(N_TEST):
        plane = my_xh if number % 2 == 0 else 1 - my_xh
        origin = plane * N_Y + (my_y + OFFSETS[number // 2] + N_Y) % N_Y
        rows_of.append(pl.multiple_of(origin * CHUNK, CHUNK))

    def build(member):
        for number in range(N_TEST):
            row = rows_of[number]
            piece_copies[member, number].wait()
            for kind in range(2):
                base = base_ref[kind, pl.ds(row, CHUNK), :].astype(jnp.float32)
                change = piece_refs[number][member, kind].astype(jnp.float32)
                for step in range(STEPS):
                    value = (base + strength_ref[0, step * MUT_DEV + member] * change).astype(jnp.bfloat16)
                    if kind == 0:
                        first_refs[member % 2][pl.ds(row, CHUNK), step * B : (step + 1) * B] = value
                    else:
                        last_refs[member % 2][step, pl.ds(row, CHUNK), :] = value

    build(0)
    pooled_ref[...] = jnp.zeros_like(pooled_ref)
    label_ref[...] = jnp.zeros_like(label_ref)
    sublane = lax.broadcasted_iota(jnp.int32, (8, B), 0)
    for variant in range(MUT_DEV):
        for entry in range(SURV):
            odd = plan_ref[1, variant * SURV + entry]
            keep_ref[variant, 0, entry] = jnp.where(sublane >= odd * 4, 1.0, 0.0)
            keep_ref[variant, 1, entry] = jnp.where(sublane < 4 + odd * 4, 1.0, 0.0)
            label = plan_ref[2, variant * SURV + entry]
            for step in range(STEPS):
                row = (variant * STEPS + step) * 16 + entry
                label_ref[row : row + 1, :] = jnp.full((1, 128), label, jnp.int32)

    for member in range(MUT_DEV):
        pltpu.make_async_copy(
            images_ref.at[pl.ds(0, ROWS)], x_ref.at[member], image_sem.at[member]
        ).wait()
        if member + 1 < MUT_DEV:
            build(member + 1)
        both = jnp.maximum(
            jnp.dot(x_ref[member], first_refs[member % 2][...], preferred_element_type=jnp.float32),
            0.0,
        ).astype(jnp.bfloat16)
        for step in range(STEPS):
            hidden = both[:, step * B : (step + 1) * B]
            for part in range(C // B):
                columns = slice(part * B, (part + 1) * B)
                expanded = lax.dot_general(
                    hidden,
                    last_refs[member % 2][step, columns, :],
                    (((1,), (1,)), ((), ())),
                    preferred_element_type=jnp.float32,
                )
                out_rows = jnp.maximum(expanded + x_ref[member, :, columns].astype(jnp.float32), 0.0)
                tiles = out_rows.reshape(SURV, SLOT // 8, 8, B)
                total = (
                    tiles[:, 0] * keep_ref[member, 0]
                    + tiles[:, 1]
                    + tiles[:, 2]
                    + tiles[:, 3] * keep_ref[member, 1]
                )
                pooled = (jnp.sum(total, axis=1) / PIX).astype(jnp.bfloat16)
                pooled_ref[member * STEPS + step, :SURV, columns] = pooled

    pltpu.make_async_copy(readout_hbm_ref, readout_ref, readout_sem).wait()
    logits = lax.dot_general(
        pooled_ref[...].reshape(MUT_DEV * STEPS * 16, C),
        readout_ref[...],
        (((1,), (1,)), ((), ())),
        preferred_element_type=jnp.float32,
    )
    top = jnp.max(logits, axis=1, keepdims=True)
    total = top + jnp.log(jnp.sum(jnp.exp(logits - top), axis=1, keepdims=True))
    column = lax.broadcasted_iota(jnp.int32, logits.shape, 1)
    chosen = jnp.sum(jnp.where(column == label_ref[:, :1], logits, 0.0), axis=1, keepdims=True)
    kill = total - chosen
    shape = (MUT_DEV * STEPS * 16, 128)
    diagonal = lax.broadcasted_iota(jnp.int32, shape, 1) == (
        lax.broadcasted_iota(jnp.int32, shape, 0) % 16
    )
    spread = jnp.where(diagonal, jnp.broadcast_to(kill, shape), 0.0)
    lined = jnp.sum(spread.reshape(MUT_DEV * STEPS, 16, 128), axis=1)
    for variant in range(MUT_DEV):
        out_ref[variant] = lined[variant * STEPS : (variant + 1) * STEPS, :SURV]


def run_score(plan, strength, images, readout, bases, pieces):
    smem = pl.BlockSpec(memory_space=pltpu.SMEM)
    vmem = pl.BlockSpec(memory_space=pltpu.VMEM)
    hbm = pl.BlockSpec(memory_space=pl.ANY)
    return pl.pallas_call(
        score,
        in_specs=[smem, smem, hbm, hbm, vmem] + [hbm] * N_TEST,
        out_specs=vmem,
        out_shape=jax.ShapeDtypeStruct((MUT_DEV, STEPS, SURV), jnp.float32),
        scratch_shapes=[
            pltpu.VMEM((MUT_DEV, ROWS, C), jnp.bfloat16),
            pltpu.VMEM((MUT_DEV * STEPS, 16, C), jnp.bfloat16),
            pltpu.VMEM((MUT_DEV, 2, SURV, 8, B), jnp.float32),
            pltpu.VMEM((MUT_DEV * STEPS * 16, 128), jnp.int32),
            pltpu.VMEM((readout.shape[0], C), jnp.bfloat16),
            pltpu.VMEM((C, STEPS * B), jnp.bfloat16),
            pltpu.VMEM((C, STEPS * B), jnp.bfloat16),
            pltpu.VMEM((STEPS, C, B), jnp.bfloat16),
            pltpu.VMEM((STEPS, C, B), jnp.bfloat16),
        ]
        + [pltpu.VMEM((MUT_DEV, 2, CHUNK, B), jnp.bfloat16)] * N_TEST
        + [
            pltpu.SemaphoreType.DMA((MUT_DEV,)),
            pltpu.SemaphoreType.DMA,
            pltpu.SemaphoreType.DMA((MUT_DEV, N_TEST)),
        ],
        compiler_params=pltpu.CompilerParams(vmem_limit_bytes=30 * 2**20),
    )(
        plan,
        strength,
        in_hbm(images),
        in_hbm(readout),
        in_vmem(bases),
        *[in_hbm(value) for value in pieces],
    )


def on_device(
    input_activation,
    ground_truth_class,
    remaining_pictures,
    learned_narrowing_kernel,
    learned_widening_kernel,
    narrowing_perturbation,
    widening_perturbation,
    perturbation_strength,
    readout_matrix,
):
    swap = [(0, 1), (1, 0)]
    up = [(i, (i + 1) % N_Y) for i in range(N_Y)]
    down = [(i, (i - 1) % N_Y) for i in range(N_Y)]

    own_rows = input_activation.reshape(IMG_DEV * PIX, C)
    message = jnp.stack(
        [narrowing_perturbation, jnp.transpose(widening_perturbation, (0, 2, 1))], axis=1
    )
    partner_rows = lax.ppermute(own_rows, "xl", swap)
    wanted = remaining_pictures.reshape(1, -1)
    holder = wanted // IMG_DEV
    within = wanted % IMG_DEV
    slot = (holder // 16 != lax.axis_index("xl")).astype(jnp.int32)
    start = (
        ((holder % 16) * 2 + slot) * (IMG_DEV * PIX) + (within // 2) * (2 * PIX) + (within % 2) * 24
    )
    shard = lax.axis_index("xh") * N_Y + lax.axis_index("y")
    label = jnp.take(ground_truth_class, (holder * N_TEST + shard) * IMG_DEV + within)
    plan = jnp.concatenate([start, within % 2, label])
    strength = jnp.pad(perturbation_strength.T.reshape(1, -1), ((0, 0), (0, 120)))
    bases = jnp.stack([learned_narrowing_kernel, learned_widening_kernel.T])
    partner_rows, message, plan, strength, bases = lax.optimization_barrier(
        (partner_rows, message, plan, strength, bases)
    )
    images = lax.all_gather(
        jnp.concatenate([own_rows, partner_rows]), ("z", "core"), axis=0, tiled=True
    )

    other = lax.ppermute(message, "xh", swap)
    first_up = lax.ppermute(message, "y", up)
    first_down = lax.ppermute(message, "y", down)
    other, first_down = lax.optimization_barrier((other, first_down))
    flows = []
    for number, seed in enumerate((message, other)):
        rising = [first_up if number == 0 else lax.ppermute(seed, "y", up)]
        falling = [first_down if number == 0 else lax.ppermute(seed, "y", down)]
        for _ in range(2):
            rising.append(lax.ppermute(rising[-1], "y", up))
            falling.append(lax.ppermute(falling[-1], "y", down))
        if number == 0:
            farthest = lax.ppermute(rising[-1], "y", up)
        else:
            farthest = lax.ppermute(falling[-1], "y", down)
        flows.append([seed] + rising + falling + [farthest])
    pieces = [flows[number % 2][number // 2] for number in range(N_TEST)]

    return run_score(plan, strength, images, readout_matrix.T, bases, pieces)


def solution(mesh):
    fine = Mesh(mesh.devices.reshape(2, 8, 2, 2, N_Y), ("xl", "z", "core", "xh", "y"))
    mut = ("xl", "z", "core")
    test = ("xh", "y")
    return jax.shard_map(
        on_device,
        mesh=fine,
        in_specs=(
            P(mut + test, None, None),
            P(),
            P(mut, test),
            P(),
            P(),
            P(mut, test, None),
            P(mut, None, test),
            P(mut, None),
            P(),
        ),
        out_specs=P(mut, None, test),
        check_vma=False,
    )
```

```python
import jax
import jax.numpy as jnp
from jax import lax
from jax.experimental import pallas as pl
from jax.experimental.pallas import tpu as pltpu
from jax.sharding import Mesh, PartitionSpec as P

N_Y = 8
N_TEST = 16
IMG_DEV = 4
PIX = 28
SLOT = 32
SURV = 14
MUT_DEV = 4
STEPS = 2
C = 1024
B = 256
CHUNK = C // N_TEST
ROWS = SURV * SLOT
LATE = (7, 12, 14, 15)
OFFSETS = (0, -1, -2, -3, 1, 2, 3, 4)


def in_hbm(value):
    return pltpu.with_memory_space_constraint(value, pltpu.HBM)


def in_vmem(value):
    return pltpu.with_memory_space_constraint(value, pltpu.VMEM)


def score(*refs):
    plan_ref, strength_ref, images_ref, readout_hbm_ref, base_ref = refs[:5]
    piece_hbm_refs = refs[5 : 5 + N_TEST]
    out_ref = refs[5 + N_TEST]
    x_ref, pooled_ref, keep_ref, label_ref, readout_ref = refs[6 + N_TEST : 11 + N_TEST]
    first_refs = refs[11 + N_TEST : 13 + N_TEST]
    last_refs = refs[13 + N_TEST : 15 + N_TEST]
    piece_refs = refs[15 + N_TEST : 15 + 2 * N_TEST]
    image_sem, readout_sem, piece_sem = refs[15 + 2 * N_TEST :]
    my_xh = lax.axis_index("xh")
    my_y = lax.axis_index("y")

    def fetch(variant):
        for entry in range(SURV):
            start = pl.multiple_of(plan_ref[0, variant * SURV + entry], 8)
            pltpu.make_async_copy(
                images_ref.at[pl.ds(start, SLOT)],
                x_ref.at[variant, pl.ds(entry * SLOT, SLOT)],
                image_sem.at[variant],
            ).start()

    piece_copies = {}
    for variant in range(MUT_DEV):
        for number in range(N_TEST):
            copy = pltpu.make_async_copy(
                piece_hbm_refs[number].at[variant],
                piece_refs[number].at[variant],
                piece_sem.at[variant, number],
            )
            copy.start()
            piece_copies[variant, number] = copy
        fetch(variant)
    pltpu.make_async_copy(readout_hbm_ref, readout_ref, readout_sem).start()

    rows_of = []
    for number in range(N_TEST):
        plane = my_xh if number % 2 == 0 else 1 - my_xh
        origin = plane * N_Y + (my_y + OFFSETS[number // 2] + N_Y) % N_Y
        rows_of.append(pl.multiple_of(origin * CHUNK, CHUNK))

    def build(member):
        for number in range(N_TEST):
            row = rows_of[number]
            piece_copies[member, number].wait()
            for kind in range(2):
                base = base_ref[kind, pl.ds(row, CHUNK), :].astype(jnp.float32)
                change = piece_refs[number][member, kind].astype(jnp.float32)
                for step in range(STEPS):
                    value = (base + strength_ref[0, step * MUT_DEV + member] * change).astype(jnp.bfloat16)
                    if kind == 0:
                        first_refs[member % 2][pl.ds(row, CHUNK), step * B : (step + 1) * B] = value
                    else:
                        last_refs[member % 2][step, pl.ds(row, CHUNK), :] = value

    build(0)
    pooled_ref[...] = jnp.zeros_like(pooled_ref)
    label_ref[...] = jnp.zeros_like(label_ref)
    sublane = lax.broadcasted_iota(jnp.int32, (8, B), 0)
    for variant in range(MUT_DEV):
        for entry in range(SURV):
            odd = plan_ref[1, variant * SURV + entry]
            keep_ref[variant, 0, entry] = jnp.where(sublane >= odd * 4, 1.0, 0.0)
            keep_ref[variant, 1, entry] = jnp.where(sublane < 4 + odd * 4, 1.0, 0.0)
            label = plan_ref[2, variant * SURV + entry]
            for step in range(STEPS):
                row = (variant * STEPS + step) * 16 + entry
                label_ref[row : row + 1, :] = jnp.full((1, 128), label, jnp.int32)

    for member in range(MUT_DEV):
        pltpu.make_async_copy(
            images_ref.at[pl.ds(0, ROWS)], x_ref.at[member], image_sem.at[member]
        ).wait()
        if member + 1 < MUT_DEV:
            build(member + 1)
        both = jnp.maximum(
            jnp.dot(x_ref[member], first_refs[member % 2][...], preferred_element_type=jnp.float32),
            0.0,
        ).astype(jnp.bfloat16)
        for step in range(STEPS):
            hidden = both[:, step * B : (step + 1) * B]
            for part in range(C // B):
                columns = slice(part * B, (part + 1) * B)
                expanded = lax.dot_general(
                    hidden,
                    last_refs[member % 2][step, columns, :],
                    (((1,), (1,)), ((), ())),
                    preferred_element_type=jnp.float32,
                )
                out_rows = jnp.maximum(expanded + x_ref[member, :, columns].astype(jnp.float32), 0.0)
                tiles = out_rows.reshape(SURV, SLOT // 8, 8, B)
                total = (
                    tiles[:, 0] * keep_ref[member, 0]
                    + tiles[:, 1]
                    + tiles[:, 2]
                    + tiles[:, 3] * keep_ref[member, 1]
                )
                pooled = (jnp.sum(total, axis=1) / PIX).astype(jnp.bfloat16)
                pooled_ref[member * STEPS + step, :SURV, columns] = pooled

    pltpu.make_async_copy(readout_hbm_ref, readout_ref, readout_sem).wait()
    logits = lax.dot_general(
        pooled_ref[...].reshape(MUT_DEV * STEPS * 16, C),
        readout_ref[...],
        (((1,), (1,)), ((), ())),
        preferred_element_type=jnp.float32,
    )
    top = jnp.max(logits, axis=1, keepdims=True)
    total = top + jnp.log(jnp.sum(jnp.exp(logits - top), axis=1, keepdims=True))
    column = lax.broadcasted_iota(jnp.int32, logits.shape, 1)
    chosen = jnp.sum(jnp.where(column == label_ref[:, :1], logits, 0.0), axis=1, keepdims=True)
    kill = total - chosen
    shape = (MUT_DEV * STEPS * 16, 128)
    diagonal = lax.broadcasted_iota(jnp.int32, shape, 1) == (
        lax.broadcasted_iota(jnp.int32, shape, 0) % 16
    )
    spread = jnp.where(diagonal, jnp.broadcast_to(kill, shape), 0.0)
    lined = jnp.sum(spread.reshape(MUT_DEV * STEPS, 16, 128), axis=1)
    for variant in range(MUT_DEV):
        out_ref[variant] = lined[variant * STEPS : (variant + 1) * STEPS, :SURV]


def run_score(plan, strength, images, readout, bases, pieces):
    smem = pl.BlockSpec(memory_space=pltpu.SMEM)
    vmem = pl.BlockSpec(memory_space=pltpu.VMEM)
    hbm = pl.BlockSpec(memory_space=pl.ANY)
    return pl.pallas_call(
        score,
        in_specs=[smem, smem, hbm, hbm, vmem] + [hbm] * N_TEST,
        out_specs=vmem,
        out_shape=jax.ShapeDtypeStruct((MUT_DEV, STEPS, SURV), jnp.float32),
        scratch_shapes=[
            pltpu.VMEM((MUT_DEV, ROWS, C), jnp.bfloat16),
            pltpu.VMEM((MUT_DEV * STEPS, 16, C), jnp.bfloat16),
            pltpu.VMEM((MUT_DEV, 2, SURV, 8, B), jnp.float32),
            pltpu.VMEM((MUT_DEV * STEPS * 16, 128), jnp.int32),
            pltpu.VMEM((readout.shape[0], C), jnp.bfloat16),
            pltpu.VMEM((C, STEPS * B), jnp.bfloat16),
            pltpu.VMEM((C, STEPS * B), jnp.bfloat16),
            pltpu.VMEM((STEPS, C, B), jnp.bfloat16),
            pltpu.VMEM((STEPS, C, B), jnp.bfloat16),
        ]
        + [pltpu.VMEM((MUT_DEV, 2, CHUNK, B), jnp.bfloat16)] * N_TEST
        + [
            pltpu.SemaphoreType.DMA((MUT_DEV,)),
            pltpu.SemaphoreType.DMA,
            pltpu.SemaphoreType.DMA((MUT_DEV, N_TEST)),
        ],
        compiler_params=pltpu.CompilerParams(vmem_limit_bytes=30 * 2**20),
    )(
        plan,
        strength,
        in_hbm(images),
        in_hbm(readout),
        in_vmem(bases),
        *[value if number in LATE else in_hbm(value) for number, value in enumerate(pieces)],
    )


def on_device(
    input_activation,
    ground_truth_class,
    remaining_pictures,
    learned_narrowing_kernel,
    learned_widening_kernel,
    narrowing_perturbation,
    widening_perturbation,
    perturbation_strength,
    readout_matrix,
):
    swap = [(0, 1), (1, 0)]
    up = [(i, (i + 1) % N_Y) for i in range(N_Y)]
    down = [(i, (i - 1) % N_Y) for i in range(N_Y)]

    own_rows = input_activation.reshape(IMG_DEV * PIX, C)
    message = jnp.stack(
        [narrowing_perturbation, jnp.transpose(widening_perturbation, (0, 2, 1))], axis=1
    )
    partner_rows = lax.ppermute(own_rows, "xl", swap)
    wanted = remaining_pictures.reshape(1, -1)
    holder = wanted // IMG_DEV
    within = wanted % IMG_DEV
    slot = (holder // 16 != lax.axis_index("xl")).astype(jnp.int32)
    start = (
        ((holder % 16) * 2 + slot) * (IMG_DEV * PIX) + (within // 2) * (2 * PIX) + (within % 2) * 24
    )
    shard = lax.axis_index("xh") * N_Y + lax.axis_index("y")
    label = jnp.take(ground_truth_class, (holder * N_TEST + shard) * IMG_DEV + within)
    plan = jnp.concatenate([start, within % 2, label])
    strength = jnp.pad(perturbation_strength.T.reshape(1, -1), ((0, 0), (0, 120)))
    bases = jnp.stack([learned_narrowing_kernel, learned_widening_kernel.T])
    partner_rows, message, plan, strength, bases = lax.optimization_barrier(
        (partner_rows, message, plan, strength, bases)
    )
    images = lax.all_gather(
        jnp.concatenate([own_rows, partner_rows]), ("z", "core"), axis=0, tiled=True
    )

    other = lax.ppermute(message, "xh", swap)
    first_up = lax.ppermute(message, "y", up)
    first_down = lax.ppermute(message, "y", down)
    other, first_down = lax.optimization_barrier((other, first_down))
    flows = []
    for number, seed in enumerate((message, other)):
        rising = [first_up if number == 0 else lax.ppermute(seed, "y", up)]
        falling = [first_down if number == 0 else lax.ppermute(seed, "y", down)]
        for _ in range(2):
            rising.append(lax.ppermute(rising[-1], "y", up))
            falling.append(lax.ppermute(falling[-1], "y", down))
        if number == 0:
            farthest = lax.ppermute(rising[-1], "y", up)
        else:
            farthest = lax.ppermute(falling[-1], "y", down)
        flows.append([seed] + rising + falling + [farthest])
    pieces = [flows[number % 2][number // 2] for number in range(N_TEST)]

    return run_score(plan, strength, images, readout_matrix.T, bases, pieces)


def solution(mesh):
    fine = Mesh(mesh.devices.reshape(2, 8, 2, 2, N_Y), ("xl", "z", "core", "xh", "y"))
    mut = ("xl", "z", "core")
    test = ("xh", "y")
    return jax.shard_map(
        on_device,
        mesh=fine,
        in_specs=(
            P(mut + test, None, None),
            P(),
            P(mut, test),
            P(),
            P(),
            P(mut, test, None),
            P(mut, None, test),
            P(mut, None),
            P(),
        ),
        out_specs=P(mut, None, test),
        check_vma=False,
    )
```

```python
import jax
import jax.numpy as jnp
from jax import lax
from jax.experimental import pallas as pl
from jax.experimental.pallas import tpu as pltpu
from jax.sharding import Mesh, PartitionSpec as P

N_Y = 8
N_TEST = 16
IMG_DEV = 4
PIX = 28
SLOT = 32
SURV = 14
MUT_DEV = 4
STEPS = 2
C = 1024
B = 256
CHUNK = C // N_TEST
ROWS = SURV * SLOT
LATE = (7, 12, 14, 15)
OFFSETS = (0, -1, -2, -3, 1, 2, 3, 4)


def in_hbm(value):
    return pltpu.with_memory_space_constraint(value, pltpu.HBM)


def in_vmem(value):
    return pltpu.with_memory_space_constraint(value, pltpu.VMEM)


def score(*refs):
    plan_ref, strength_ref, images_ref, readout_hbm_ref, base_ref = refs[:5]
    piece_hbm_refs = refs[5 : 5 + N_TEST]
    out_ref = refs[5 + N_TEST]
    x_ref, pooled_ref, keep_ref, label_ref, readout_ref = refs[6 + N_TEST : 11 + N_TEST]
    first_refs = refs[11 + N_TEST : 13 + N_TEST]
    last_refs = refs[13 + N_TEST : 15 + N_TEST]
    piece_refs = refs[15 + N_TEST : 15 + 2 * N_TEST]
    image_sem, readout_sem, piece_sem = refs[15 + 2 * N_TEST :]
    my_xh = lax.axis_index("xh")
    my_y = lax.axis_index("y")

    def fetch(variant):
        for entry in range(SURV):
            start = pl.multiple_of(plan_ref[0, variant * SURV + entry], 8)
            pltpu.make_async_copy(
                images_ref.at[pl.ds(start, SLOT)],
                x_ref.at[variant, pl.ds(entry * SLOT, SLOT)],
                image_sem.at[variant],
            ).start()

    piece_copies = {}
    for variant in range(MUT_DEV):
        for number in range(N_TEST):
            copy = pltpu.make_async_copy(
                piece_hbm_refs[number].at[variant],
                piece_refs[number].at[variant],
                piece_sem.at[variant, number],
            )
            copy.start()
            piece_copies[variant, number] = copy
        fetch(variant)
    pltpu.make_async_copy(readout_hbm_ref, readout_ref, readout_sem).start()

    rows_of = []
    for number in range(N_TEST):
        plane = my_xh if number % 2 == 0 else 1 - my_xh
        origin = plane * N_Y + (my_y + OFFSETS[number // 2] + N_Y) % N_Y
        rows_of.append(pl.multiple_of(origin * CHUNK, CHUNK))

    def build(member):
        for number in range(N_TEST):
            row = rows_of[number]
            piece_copies[member, number].wait()
            for kind in range(2):
                base = base_ref[kind, pl.ds(row, CHUNK), :].astype(jnp.float32)
                change = piece_refs[number][member, kind].astype(jnp.float32)
                for step in range(STEPS):
                    value = (base + strength_ref[0, step * MUT_DEV + member] * change).astype(jnp.bfloat16)
                    if kind == 0:
                        first_refs[member % 2][pl.ds(row, CHUNK), step * B : (step + 1) * B] = value
                    else:
                        last_refs[member % 2][step, pl.ds(row, CHUNK), :] = value

    build(0)
    pooled_ref[...] = jnp.zeros_like(pooled_ref)
    label_ref[...] = jnp.zeros_like(label_ref)
    sublane = lax.broadcasted_iota(jnp.int32, (8, B), 0)
    for variant in range(MUT_DEV):
        for entry in range(SURV):
            odd = plan_ref[1, variant * SURV + entry]
            keep_ref[variant, 0, entry] = jnp.where(sublane >= odd * 4, 1.0, 0.0)
            keep_ref[variant, 1, entry] = jnp.where(sublane < 4 + odd * 4, 1.0, 0.0)
            label = plan_ref[2, variant * SURV + entry]
            for step in range(STEPS):
                row = (variant * STEPS + step) * 16 + entry
                label_ref[row : row + 1, :] = jnp.full((1, 128), label, jnp.int32)

    for member in range(MUT_DEV):
        pltpu.make_async_copy(
            images_ref.at[pl.ds(0, ROWS)], x_ref.at[member], image_sem.at[member]
        ).wait()
        if member + 1 < MUT_DEV:
            build(member + 1)
        both = jnp.maximum(
            jnp.dot(x_ref[member], first_refs[member % 2][...], preferred_element_type=jnp.float32),
            0.0,
        ).astype(jnp.bfloat16)
        for step in range(STEPS):
            hidden = both[:, step * B : (step + 1) * B]
            for part in range(C // B):
                columns = slice(part * B, (part + 1) * B)
                expanded = lax.dot_general(
                    hidden,
                    last_refs[member % 2][step, columns, :],
                    (((1,), (1,)), ((), ())),
                    preferred_element_type=jnp.float32,
                )
                out_rows = jnp.maximum(expanded + x_ref[member, :, columns].astype(jnp.float32), 0.0)
                tiles = out_rows.reshape(SURV, SLOT // 8, 8, B)
                total = (
                    tiles[:, 0] * keep_ref[member, 0]
                    + tiles[:, 1]
                    + tiles[:, 2]
                    + tiles[:, 3] * keep_ref[member, 1]
                )
                pooled = (jnp.sum(total, axis=1) / PIX).astype(jnp.bfloat16)
                pooled_ref[member * STEPS + step, :SURV, columns] = pooled

    pltpu.make_async_copy(readout_hbm_ref, readout_ref, readout_sem).wait()
    logits = lax.dot_general(
        pooled_ref[...].reshape(MUT_DEV * STEPS * 16, C),
        readout_ref[...],
        (((1,), (1,)), ((), ())),
        preferred_element_type=jnp.float32,
    )
    top = jnp.max(logits, axis=1, keepdims=True)
    total = top + jnp.log(jnp.sum(jnp.exp(logits - top), axis=1, keepdims=True))
    column = lax.broadcasted_iota(jnp.int32, logits.shape, 1)
    chosen = jnp.sum(jnp.where(column == label_ref[:, :1], logits, 0.0), axis=1, keepdims=True)
    kill = total - chosen
    shape = (MUT_DEV * STEPS * 16, 128)
    diagonal = lax.broadcasted_iota(jnp.int32, shape, 1) == (
        lax.broadcasted_iota(jnp.int32, shape, 0) % 16
    )
    spread = jnp.where(diagonal, jnp.broadcast_to(kill, shape), 0.0)
    lined = jnp.sum(spread.reshape(MUT_DEV * STEPS, 16, 128), axis=1)
    for variant in range(MUT_DEV):
        out_ref[variant] = lined[variant * STEPS : (variant + 1) * STEPS, :SURV]


def run_score(plan, strength, images, readout, bases, pieces):
    smem = pl.BlockSpec(memory_space=pltpu.SMEM)
    vmem = pl.BlockSpec(memory_space=pltpu.VMEM)
    hbm = pl.BlockSpec(memory_space=pl.ANY)
    return pl.pallas_call(
        score,
        in_specs=[smem, smem, hbm, hbm, vmem] + [hbm] * N_TEST,
        out_specs=vmem,
        out_shape=jax.ShapeDtypeStruct((MUT_DEV, STEPS, SURV), jnp.float32),
        scratch_shapes=[
            pltpu.VMEM((MUT_DEV, ROWS, C), jnp.bfloat16),
            pltpu.VMEM((MUT_DEV * STEPS, 16, C), jnp.bfloat16),
            pltpu.VMEM((MUT_DEV, 2, SURV, 8, B), jnp.float32),
            pltpu.VMEM((MUT_DEV * STEPS * 16, 128), jnp.int32),
            pltpu.VMEM((readout.shape[0], C), jnp.bfloat16),
            pltpu.VMEM((C, STEPS * B), jnp.bfloat16),
            pltpu.VMEM((C, STEPS * B), jnp.bfloat16),
            pltpu.VMEM((STEPS, C, B), jnp.bfloat16),
            pltpu.VMEM((STEPS, C, B), jnp.bfloat16),
        ]
        + [pltpu.VMEM((MUT_DEV, 2, CHUNK, B), jnp.bfloat16)] * N_TEST
        + [
            pltpu.SemaphoreType.DMA((MUT_DEV,)),
            pltpu.SemaphoreType.DMA,
            pltpu.SemaphoreType.DMA((MUT_DEV, N_TEST)),
        ],
        compiler_params=pltpu.CompilerParams(vmem_limit_bytes=30 * 2**20),
    )(
        plan,
        strength,
        in_hbm(images),
        in_hbm(readout),
        in_vmem(bases),
        *[value if number in LATE else in_hbm(value) for number, value in enumerate(pieces)],
    )


def on_device(
    input_activation,
    ground_truth_class,
    remaining_pictures,
    learned_narrowing_kernel,
    learned_widening_kernel,
    narrowing_perturbation,
    widening_perturbation,
    perturbation_strength,
    readout_matrix,
):
    swap = [(0, 1), (1, 0)]
    up = [(i, (i + 1) % N_Y) for i in range(N_Y)]
    down = [(i, (i - 1) % N_Y) for i in range(N_Y)]

    own_rows = input_activation.reshape(IMG_DEV * PIX, C)
    message = jnp.stack(
        [narrowing_perturbation, jnp.transpose(widening_perturbation, (0, 2, 1))], axis=1
    )
    partner_rows = lax.ppermute(own_rows, "xl", swap)
    wanted = remaining_pictures.reshape(1, -1)
    holder = wanted // IMG_DEV
    within = wanted % IMG_DEV
    slot = (holder // 16 != lax.axis_index("xl")).astype(jnp.int32)
    start = (
        ((holder % 16) * 2 + slot) * (IMG_DEV * PIX) + (within // 2) * (2 * PIX) + (within % 2) * 24
    )
    shard = lax.axis_index("xh") * N_Y + lax.axis_index("y")
    label = jnp.take(ground_truth_class, (holder * N_TEST + shard) * IMG_DEV + within)
    plan = jnp.concatenate([start, within % 2, label])
    strength = jnp.pad(perturbation_strength.T.reshape(1, -1), ((0, 0), (0, 120)))
    bases = jnp.stack([learned_narrowing_kernel, learned_widening_kernel.T])
    partner_rows, message, plan, strength, bases = lax.optimization_barrier(
        (partner_rows, message, plan, strength, bases)
    )
    images = lax.all_gather(
        jnp.concatenate([own_rows, partner_rows]), ("z", "core"), axis=0, tiled=True
    )

    other = lax.ppermute(message, "xh", swap)
    first_up = lax.ppermute(message, "y", up)
    first_down = lax.ppermute(message, "y", down)
    flows = []
    for number, seed in enumerate((message, other)):
        rising = [first_up if number == 0 else lax.ppermute(seed, "y", up)]
        falling = [first_down if number == 0 else lax.ppermute(seed, "y", down)]
        for _ in range(2):
            rising.append(lax.ppermute(rising[-1], "y", up))
            falling.append(lax.ppermute(falling[-1], "y", down))
        if number == 0:
            farthest = lax.ppermute(rising[-1], "y", up)
        else:
            farthest = lax.ppermute(falling[-1], "y", down)
        flows.append([seed] + rising + falling + [farthest])
    pieces = [flows[number % 2][number // 2] for number in range(N_TEST)]

    return run_score(plan, strength, images, readout_matrix.T, bases, pieces)


def solution(mesh):
    fine = Mesh(mesh.devices.reshape(2, 8, 2, 2, N_Y), ("xl", "z", "core", "xh", "y"))
    mut = ("xl", "z", "core")
    test = ("xh", "y")
    return jax.shard_map(
        on_device,
        mesh=fine,
        in_specs=(
            P(mut + test, None, None),
            P(),
            P(mut, test),
            P(),
            P(),
            P(mut, test, None),
            P(mut, None, test),
            P(mut, None),
            P(),
        ),
        out_specs=P(mut, None, test),
        check_vma=False,
    )
```
